32 devices in a mesh: tile: 8 (over z, x), tp: 4 (over y, core).
Axes of the slice: x: 2, y: 2, z: 4, core: 2. Of those that a mesh axis runs over, the one named last changes fastest.
Arguments:
- latent: bfloat16 [512, 1024], P(('tile', 'tp')), may hold values from -6 to 6
- weight_in: bfloat16 [1024, 4096], P(None, 'tp'), may hold values from -0.1875 to 0.1875
- weight_out: bfloat16 [4096, 1024], P('tp'), may hold values from -0.09375 to 0.09375
- weight_conv: bfloat16 [7168, 2048], P(None, 'tp'), may hold values from -0.0625 to 0.0625
- neighbours: int32 [512, 7], P('tile'), may hold values from 0 to 96, as said below
- child_order: int32 [2048], P(('tile', 'tp')), may hold values from 0 to 63, as said below
- cotangent: bfloat16 [2048, 512], P(('tile', 'tp')), may hold values from -6 to 6
Outputs:
- fine_cells: bfloat16 [2048, 512], P(('tile', 'tp'))
- grad_latent: float32 [512, 1024], P(('tile', 'tp'))
- weight_in_grad: float32 [1024, 4096], P('tile', 'tp')
- weight_out_grad: float32 [4096, 1024], P('tp', 'tile')
- weight_conv_grad: float32 [7168, 2048], P('tile', 'tp')
The draws below stay inside these ranges and needn't reach their ends.
Inputs may be any that keep to these rules, and one draw needn't show every extreme that they name: `neighbours`: column 0 of the row of a tile's i-th cell is i + 16 (the cell itself); the other columns lie within 16 of it, except that index 96, the empty row, marks a missing sixth neighbour of a pentagon cell. `child_order`: each block of 64 consecutive entries is a permutation of 0 .. 63.
All inputs are finite; a program needn't handle non-finite values.
Results may differ from the reference program's by a relative error of at most 0.02.
Values may be sent and summed in bfloat16 or wider, within the bound.
No kernel may reach another device: no remote copies, remote signals or barrier semaphores. Data moves between devices by JAX's collectives and lax.ppermute only.
A program may use at most 128 MiB of HBM per device.

```python
import jax
import jax.numpy as jnp
from jax import lax

D = 1024
FF = 4096
C1 = 512
TAPS = 7
SLOTS = 4
HALO = 16
SUB = 16
TILE_CELLS = 64
COARSE = 512
FINE = 2048
N_TILE = 8
N_TP = 4


def draw_neighbours(key, part):
    row_ids = jnp.arange(COARSE, dtype=jnp.int32)
    local_ids = row_ids % TILE_CELLS + HALO
    offsets = jax.random.randint(jax.random.fold_in(key, 1), (COARSE, TAPS - 1), -HALO, HALO + 1, dtype=jnp.int32)
    beside_all = local_ids[:, None] + offsets
    empty_row = TILE_CELLS + 2 * HALO
    pentagon = jax.random.randint(jax.random.fold_in(key, 2), (COARSE,), 0, 12, dtype=jnp.int32) == 0
    last_column = jnp.where(pentagon, empty_row, beside_all[:, TAPS - 2])
    beside_all = jnp.concatenate([beside_all[:, :TAPS - 2], last_column[:, None]], axis=1)
    beside_all = beside_all.at[0, 0].set(0).at[0, TAPS - 2].set(empty_row)
    return jnp.concatenate([local_ids[:, None], beside_all], axis=1).astype(jnp.int32)


def draw_child_order(key, part):
    block_rows = SLOTS * SUB
    keys_all = jax.random.split(key, FINE // block_rows)
    orders = jax.vmap(lambda subkey: jax.random.permutation(subkey, block_rows))(keys_all)
    return orders.reshape(FINE).astype(jnp.int32)


def block_levels(key, shape, cuts, least, largest):
    factor_of, own = 1.0, jax.random.fold_in(key, 6)
    for dim, shards_of in cuts:
        steps = jnp.exp(jax.random.uniform(jax.random.fold_in(own, dim), (shards_of,), jnp.float32, least / len(cuts), largest / len(cuts)))
        factor_of = factor_of * jnp.repeat(steps, shape[dim] // shards_of).reshape([-1 if axis == dim else 1 for axis in range(len(shape))])
    return factor_of


def noise(own_key, dims, scale, most, shards=(), held_as=jnp.bfloat16):
    values = jax.random.normal(own_key, dims, jnp.float32) * scale
    if len(shards) > 0:
        values = block_levels(own_key, dims, shards, -0.22, 0.18) * values
    return jnp.clip(values, min=-most, max=most).astype(held_as)


def setup_inputs(seed: int = 0) -> dict:
    key_of = jax.random.split(jax.random.key(seed), 8)
    latent = noise(key_of[0], (COARSE, D), 1.0, 6.0, ((0, 32),))
    weight_in = noise(key_of[1], (D, FF), D ** -0.5, 0.1875, ((1, 4),))
    weight_out = noise(key_of[2], (FF, D), FF ** -0.5, 0.09375, ((0, 4),))
    weight_conv = noise(key_of[3], (TAPS * D, C1 * SLOTS), (TAPS * D) ** -0.5, 0.0625, ((1, 4),))
    neighbours = draw_neighbours(jax.random.fold_in(key_of[7], 71), 0)
    child_order = draw_child_order(jax.random.fold_in(key_of[7], 71), 0)
    cotangent = noise(key_of[6], (FINE, C1), 1.0, 6.0, ((0, 32),))
    return {"latent": latent, "weight_in": weight_in, "weight_out": weight_out, "weight_conv": weight_conv, "neighbours": neighbours, "child_order": child_order, "cotangent": cotangent}


EPSILON = 1e-05

def silu_grad(pre_value):
    sigmoid = jax.nn.sigmoid(pre_value)
    return sigmoid * (1.0 + pre_value * (1.0 - sigmoid))

def rounded(values):
    return lax.optimization_barrier(values.astype(jnp.bfloat16)).astype(jnp.float32)

def extend(tiles):
    zeros_rim = jnp.zeros_like(tiles[:1, :HALO])
    before = jnp.concatenate([zeros_rim, tiles[:-1, TILE_CELLS - HALO:]], axis=0)
    after = jnp.concatenate([tiles[1:, :HALO], zeros_rim], axis=0)
    empty_row = jnp.zeros_like(tiles[:, :1])
    return jnp.concatenate([before, tiles, after, empty_row], axis=1)

def pick_rows(extended, picks):
    return jax.vmap(lambda table, chosen: table[chosen])(extended, picks)

def reference(latent, weight_in, weight_out, weight_conv, neighbours, child_order, cotangent):
    grad_scale = 1.0 / COARSE ** 0.5
    group_units = FF // N_TP
    group_cols = C1 * SLOTS // N_TP
    block_rows = SLOTS * SUB
    group_ids = jnp.arange(N_TP, dtype=jnp.int32)
    source = latent.astype(jnp.float32)
    norm_factor = lax.rsqrt(lax.optimization_barrier(jnp.mean(source * source, axis=1, keepdims=True)) + EPSILON)
    normed = (source * norm_factor).astype(jnp.bfloat16)
    pre_act = jnp.dot(normed, weight_in, preferred_element_type=jnp.float32)
    hidden = jax.nn.silu(pre_act).astype(jnp.bfloat16)

    def mixed_group(running, group):
        start = group * group_units
        term_part = jnp.dot(lax.dynamic_slice_in_dim(hidden, start, group_units, 1), lax.dynamic_slice_in_dim(weight_out, start, group_units, 0), preferred_element_type=jnp.float32)
        return (running + rounded(term_part), None)
    mixed, _ = lax.scan(mixed_group, jnp.zeros((COARSE, D), jnp.float32), group_ids)
    latent_out = (source + mixed).astype(jnp.bfloat16)
    extended = extend(latent_out.reshape(N_TILE, TILE_CELLS, D))
    table_index = neighbours.reshape(N_TILE, TILE_CELLS, TAPS)
    tap_rows = pick_rows(extended, table_index).reshape(COARSE, TAPS * D)
    coarse_out = jnp.dot(tap_rows, weight_conv, preferred_element_type=jnp.float32).astype(jnp.bfloat16)
    children = coarse_out.reshape(COARSE, C1, SLOTS).transpose(0, 2, 1).reshape(FINE, C1)
    activated = jax.nn.silu(children.astype(jnp.float32)).astype(jnp.bfloat16)
    order = child_order.reshape(FINE // block_rows, block_rows)
    fine_cells = jax.vmap(lambda table, chosen: table[chosen])(activated.reshape(FINE // block_rows, block_rows, C1), order).reshape(FINE, C1)
    child_grad = jax.vmap(lambda table, chosen: jnp.zeros_like(table).at[chosen].set(table))(cotangent.reshape(FINE // block_rows, block_rows, C1), order).reshape(FINE, C1)
    child_pre_grad = (child_grad.astype(jnp.float32) * silu_grad(children.astype(jnp.float32))).astype(jnp.bfloat16)
    coarse_grad = child_pre_grad.reshape(COARSE, SLOTS, C1).transpose(0, 2, 1).reshape(COARSE, C1 * SLOTS)
    flat_index = table_index.reshape(N_TILE, TILE_CELLS * TAPS)

    def latent_group(running, group):
        start = group * group_cols
        grad_cols = lax.dynamic_slice_in_dim(coarse_grad, start, group_cols, 1)
        weight_cols = lax.dynamic_slice_in_dim(weight_conv, start, group_cols, 1)
        tap_grad = jnp.dot(grad_cols, weight_cols.T, preferred_element_type=jnp.float32)
        tap_grad = tap_grad.reshape(N_TILE, TILE_CELLS * TAPS, D)
        ext_grad = jax.vmap(lambda contrib, chosen: jnp.zeros((TILE_CELLS + 2 * HALO + 1, D), jnp.float32).at[chosen].add(contrib))(tap_grad, flat_index)
        first_rim = rounded(ext_grad[:, :HALO])
        second_rim = rounded(ext_grad[:, TILE_CELLS + HALO:TILE_CELLS + 2 * HALO])
        zeros_rim = jnp.zeros_like(first_rim[:1])
        from_before = jnp.concatenate([zeros_rim, second_rim[:-1]], axis=0)
        from_after = jnp.concatenate([first_rim[1:], zeros_rim], axis=0)
        partial_value = ext_grad[:, HALO:HALO + TILE_CELLS]
        partial_value = partial_value.at[:, :HALO].add(from_before)
        partial_value = partial_value.at[:, TILE_CELLS - HALO:].add(from_after)
        return (running + rounded(partial_value.reshape(COARSE, D)), None)
    latent_grad, _ = lax.scan(latent_group, jnp.zeros((COARSE, D), jnp.float32), group_ids)
    upstream = latent_grad.astype(jnp.bfloat16)
    hidden_grad = jnp.dot(upstream, weight_out.T, preferred_element_type=jnp.float32)
    pre_grad = (hidden_grad * silu_grad(pre_act)).astype(jnp.bfloat16)

    def normed_group(running, group):
        start = group * group_units
        term_part = jnp.dot(lax.dynamic_slice_in_dim(pre_grad, start, group_units, 1), lax.dynamic_slice_in_dim(weight_in, start, group_units, 1).T, preferred_element_type=jnp.float32)
        return (running + rounded(term_part), None)
    normed_grad, _ = lax.scan(normed_group, jnp.zeros((COARSE, D), jnp.float32), group_ids)
    grad_latent = latent_grad + norm_factor * normed_grad - source * norm_factor * norm_factor * norm_factor * lax.optimization_barrier(jnp.mean(normed_grad * source, axis=1, keepdims=True))

    def tile_terms(running, pieces):
        normed_t, pre_grad_t, hidden_t, upstream_t, taps_t, coarse_t = pieces
        in_term = jnp.dot(normed_t.T, pre_grad_t, preferred_element_type=jnp.float32) * grad_scale
        out_term = jnp.dot(hidden_t.T, upstream_t, preferred_element_type=jnp.float32) * grad_scale
        conv_term = jnp.dot(taps_t.T, coarse_t, preferred_element_type=jnp.float32) * grad_scale
        return ((running[0] + rounded(in_term), running[1] + rounded(out_term), running[2] + rounded(conv_term)), None)
    pieces = tuple((array.reshape(N_TILE, TILE_CELLS, array.shape[1]) for array in (normed, pre_grad, hidden, upstream, tap_rows, coarse_grad)))
    start_sums = (jnp.zeros((D, FF), jnp.float32), jnp.zeros((FF, D), jnp.float32), jnp.zeros((TAPS * D, C1 * SLOTS), jnp.float32))
    sums, _ = lax.scan(tile_terms, start_sums, pieces)
    return (fine_cells, grad_latent, sums[0], sums[1], sums[2])
```

```python
import functools
import math

import jax
import jax.numpy as jnp
from jax import lax
from jax.experimental import pallas as pl
from jax.experimental.pallas import tpu as pltpu
from jax.sharding import PartitionSpec as P

SLOTS = 4
HALO = 16
EPSILON = 1e-05
ABSENT = 100.0
BF = jnp.bfloat16
F32 = jnp.float32


def silu_grad(pre_value):
    sigmoid = jax.nn.sigmoid(pre_value)
    return sigmoid * (1.0 + pre_value * (1.0 - sigmoid))


def dot(a, b, dims=((1,), (0,))):
    return lax.dot_general(a, b, (dims, ((), ())), preferred_element_type=F32)


def flip(value, bit):
    count = lax.axis_size("tp")
    return lax.ppermute(value, "tp", [(i, i ^ bit) for i in range(count)])


def higher_bits():
    bits, bit = [], 2
    while bit < lax.axis_size("tp"):
        bits.append(bit)
        bit *= 2
    return bits


def to_all_tiles(value):
    tiles = lax.axis_size("tile")
    copies = jnp.broadcast_to(value[None], (tiles, *value.shape))
    return lax.all_to_all(copies, "tile", split_axis=0, concat_axis=0, tiled=True)


def tap_of(table, k):
    lanes = lax.broadcasted_iota(jnp.int32, table.shape, 1)
    return jnp.sum(jnp.where(lanes == k, table, 0.0), axis=1, keepdims=True)


def conv_forward(rows_ref, table_ref, cot_ref, weight_ref, grad_ref, act_ref, acc_ref, *, halo):
    k = pl.program_id(0)

    @pl.when(k == 0)
    def _():
        acc_ref[...] = jnp.zeros_like(acc_ref)

    target = tap_of(table_ref[...], k).astype(jnp.int32)
    cells, window = acc_ref.shape[0], rows_ref.shape[0]
    pick = lax.broadcasted_iota(jnp.int32, (cells, window), 1) == target
    taps = dot(pick.astype(F32).astype(BF), rows_ref[...]).astype(BF)
    acc_ref[...] += dot(taps, weight_ref[...])

    @pl.when(k == pl.num_programs(0) - 1)
    def _():
        value = acc_ref[...].astype(BF).astype(F32)
        sigmoid = jax.nn.sigmoid(value)
        slope = sigmoid * (1.0 + value * (1.0 - sigmoid))
        grad_ref[...] = (cot_ref[...].astype(F32) * slope).astype(BF)
        act = (value * sigmoid).astype(BF)
        act_ref[...] = act[halo : cells - halo]


def conv_backward(grad_ref, table_ref, order_ref, weight_ref, out_ref, acc_ref):
    k = pl.program_id(0)

    @pl.when(k == 0)
    def _():
        acc_ref[...] = jnp.zeros_like(acc_ref)

    target = tap_of(table_ref[...], k).astype(jnp.int32)
    pick = (order_ref[0:1, :] == target).astype(F32).astype(BF)
    summed = dot(pick, grad_ref[...], ((0,), (0,))).astype(BF)
    acc_ref[...] += dot(summed, weight_ref[...], ((1,), (1,)))

    @pl.when(k == pl.num_programs(0) - 1)
    def _():
        out_ref[...] = acc_ref[...].astype(BF)


def whole(shape):
    return pl.BlockSpec(shape, lambda k: (0,) * len(shape))


def run_conv_forward(rows, table, cot, weight, features):
    cells, cols = cot.shape
    taps = weight.shape[0] // features
    return pl.pallas_call(
        functools.partial(conv_forward, halo=HALO),
        grid=(taps,),
        in_specs=[
            whole(rows.shape),
            whole(table.shape),
            whole(cot.shape),
            pl.BlockSpec((features, cols), lambda k: (k, 0)),
        ],
        out_specs=[whole((cells, cols)), whole((cells - 2 * HALO, cols))],
        out_shape=[
            jax.ShapeDtypeStruct((cells, cols), BF),
            jax.ShapeDtypeStruct((cells - 2 * HALO, cols), BF),
        ],
        scratch_shapes=[pltpu.VMEM((cells, cols), F32)],
        name="conv_forward",
    )(rows, table, cot, weight)


def run_conv_backward(grad, table, order, weight, features):
    cells, cols = grad.shape
    taps = weight.shape[0] // features
    out = (order.shape[1], features)
    return pl.pallas_call(
        conv_backward,
        grid=(taps,),
        in_specs=[
            whole(grad.shape),
            whole(table.shape),
            whole(order.shape),
            pl.BlockSpec((features, cols), lambda k: (k, 0)),
        ],
        out_specs=whole(out),
        out_shape=jax.ShapeDtypeStruct(out, BF),
        scratch_shapes=[pltpu.VMEM(out, F32)],
        name="conv_backward",
    )(grad, table, order, weight)


def local(latent, weight_in, weight_out, weight_conv, neighbours, child_order, cotangent):
    groups = lax.axis_size("tp")
    tiles = lax.axis_size("tile")
    sub, features = latent.shape
    tile_rows = sub * groups
    tap_count = neighbours.shape[1]
    cols = weight_conv.shape[1]
    chans = cols // SLOTS
    grad_scale = 1.0 / math.sqrt(tile_rows * tiles)
    member = lax.axis_index("tp")
    tile = lax.axis_index("tile")
    core = member % 2
    half = tile_rows // 2
    assert sub == HALO and groups >= 4

    row_ids = jnp.arange(tile_rows, dtype=jnp.int32)[:, None]
    offsets = jnp.where(
        neighbours == tile_rows + 2 * HALO, ABSENT, (neighbours - row_ids - HALO).astype(F32)
    )
    offsets = jnp.pad(offsets, ((0, 0), (0, 128 - tap_count))).astype(BF)
    own_offsets = lax.dynamic_slice_in_dim(offsets, member * sub, sub, 0)
    packed = jnp.concatenate([latent, own_offsets], axis=1)

    last = groups - 1
    hops = [((t + 1) * groups + p, t * groups + p) for t in range(tiles - 1) for p in (0, 1)]
    hops += [(t * groups + p, (t + 1) * groups + p) for t in range(tiles - 1) for p in (last - 1, last)]
    beside = lax.ppermute(packed, ("tile", "tp"), hops)
    blocks = lax.all_gather(jnp.concatenate([packed, beside], axis=0), "tp", axis=0, tiled=False)
    own_rows = blocks[:, :sub].reshape(tile_rows, -1)
    left = blocks[groups - 2 :, sub:].reshape(2 * sub, -1)
    right = blocks[:2, sub:].reshape(2 * sub, -1)
    window = jnp.concatenate([left, own_rows, right], axis=0)
    source = window[:, :features].astype(F32)
    cells = tile_rows + 2 * HALO
    cell_ids = jnp.arange(cells, dtype=F32)[:, None]
    table = window[HALO : HALO + cells, features:].astype(F32)
    table = jnp.where(table == ABSENT, -1.0, table + cell_ids + HALO)

    fine_rows = sub * SLOTS
    fine_ids = jnp.arange(fine_rows, dtype=jnp.int32)
    fine_of = SLOTS * (fine_ids % sub) + fine_ids // sub
    chosen = (child_order[None, :] == fine_of[:, None]).astype(BF)
    child_grad = dot(chosen, cotangent).astype(BF)
    child_hops = [h for h in hops if h[0] % groups in (0, last)]
    child_beside = lax.ppermute(child_grad, ("tile", "tp"), child_hops)
    both = jnp.stack([child_grad, child_beside])
    both = both.reshape(2 * fine_rows, groups, chans).transpose(1, 0, 2)
    arrived = lax.all_to_all(both, "tp", split_axis=0, concat_axis=0, tiled=True)
    arrived = arrived.reshape(groups, 2, SLOTS, sub, chans)
    in_order = jnp.concatenate(
        [arrived[last:, 1], arrived[:, 0], arrived[:1, 1]], axis=0
    )
    in_order = in_order.transpose(0, 2, 1, 3).reshape(cells, cols)
    col_ids = jnp.arange(cols, dtype=jnp.int32)
    col_from = (col_ids % SLOTS) * chans + col_ids // SLOTS
    reorder = (col_ids[:, None] == col_from[None, :]).astype(BF)
    cot = dot(in_order, reorder).astype(BF)

    factor = lax.rsqrt(jnp.mean(source * source, axis=1, keepdims=True) + EPSILON)
    normed = (source * factor).astype(BF)
    pre_act = dot(normed, weight_in)
    hidden = jax.nn.silu(pre_act).astype(BF)
    mixed = dot(hidden, weight_out).astype(BF)
    for bit in [1] + higher_bits():
        mixed_sum = mixed.astype(F32) + flip(mixed, bit).astype(F32)
        mixed = mixed_sum.astype(BF)
    latent_out = (source + mixed_sum).astype(BF)

    coarse_grad, activated = run_conv_forward(latent_out, table, cot, weight_conv, features)

    row_of = jnp.arange(half, dtype=jnp.int32)
    kept = (row_of // sub) * 2 * sub + row_of % sub + core * sub
    given = (row_of // sub) * 2 * sub + row_of % sub + (1 - core) * sub
    order = jnp.concatenate([kept, given])
    order_rows = jnp.broadcast_to((order + 2 * HALO)[None, :], (8, tile_rows))
    partial_value = run_conv_backward(coarse_grad, table, order_rows, weight_conv, features)

    value = partial_value[:half].astype(F32) + flip(partial_value[half:], 1).astype(F32)
    for bit in higher_bits():
        piece = value.astype(BF)
        value = piece.astype(F32) + flip(piece, bit).astype(F32)
    latent_grad = value
    upstream = latent_grad.astype(BF)
    other_upstream = flip(upstream, 1)

    def own_half(rows):
        parts = rows.reshape(groups // 2, 2, sub, rows.shape[1])
        return lax.dynamic_index_in_dim(parts, core, 1, keepdims=False).reshape(half, -1)

    def other_half(rows):
        parts = rows.reshape(groups // 2, 2, sub, rows.shape[1])
        return lax.dynamic_index_in_dim(parts, 1 - core, 1, keepdims=False).reshape(half, -1)

    packed_mine = to_all_tiles(own_half(own_rows))
    packed_other = flip(packed_mine, 1)
    out_rows = latent_out[2 * HALO : 2 * HALO + tile_rows]
    out_mine = to_all_tiles(own_half(out_rows))
    out_other = flip(out_mine, 1)
    coarse_grads = to_all_tiles(coarse_grad[HALO : HALO + tile_rows])
    up_mine = to_all_tiles(upstream)
    up_other = flip(up_mine, 1)

    own_pre = pre_act[2 * HALO : 2 * HALO + tile_rows]
    own_slope = silu_grad(jnp.concatenate([own_half(own_pre), other_half(own_pre)], axis=0))
    up_rows = jnp.concatenate([upstream, other_upstream], axis=0)
    own_pre_grad = (dot(up_rows, weight_out, ((1,), (1,))) * own_slope).astype(BF)
    normed_part = dot(own_pre_grad, weight_in, ((1,), (1,))).astype(BF)
    block = member // 2
    normed_sum = normed_part[:half].astype(F32) + flip(normed_part[half:], 1).astype(F32)
    rows_left, index = normed_sum, block
    for bit in reversed(higher_bits()):
        piece = rows_left.astype(BF)
        count = piece.shape[0] // 2
        upper = (member // bit) % 2
        keep = lax.dynamic_slice_in_dim(piece, upper * count, count, 0)
        give = lax.dynamic_slice_in_dim(piece, (1 - upper) * count, count, 0)
        rows_left = keep.astype(F32) + flip(give, bit).astype(F32)
    normed_grad = rows_left
    own_source = latent.astype(F32)
    own_factor = lax.rsqrt(jnp.mean(own_source * own_source, axis=1, keepdims=True) + EPSILON)
    own_latent_grad = lax.dynamic_slice_in_dim(latent_grad, block * sub, sub, 0)
    grad_latent = (
        own_latent_grad
        + own_factor * normed_grad
        - own_source
        * own_factor
        * own_factor
        * own_factor
        * jnp.mean(normed_grad * own_source, axis=1, keepdims=True)
    )

    by_slot = dot(activated, reorder, ((1,), (1,))).astype(BF)
    by_slot = lax.all_to_all(
        by_slot.reshape(groups, sub, cols), "tp", split_axis=0, concat_axis=0, tiled=True
    )
    children = by_slot.reshape(groups, sub, SLOTS, chans).transpose(2, 1, 0, 3)
    children = children.reshape(fine_rows, groups * chans)
    fine_cells = dot(chosen, children, ((0,), (0,))).astype(BF)

    def halves(mine, other):
        return jnp.concatenate([mine, other], axis=0).reshape(2 * tiles * half, -1)

    packed_all = halves(packed_mine, packed_other)
    source_all = packed_all[:, :features].astype(F32)
    factor_all = lax.rsqrt(jnp.mean(source_all * source_all, axis=1, keepdims=True) + EPSILON)
    normed_all = (source_all * factor_all).astype(BF)
    pre_all = dot(normed_all, weight_in)
    hidden_all = jax.nn.silu(pre_all).astype(BF)
    up_all = halves(up_mine, up_other)
    pre_grad_all = (dot(up_all, weight_out, ((1,), (1,))) * silu_grad(pre_all)).astype(BF)
    d_cols = features // tiles
    normed_cols = lax.dynamic_slice_in_dim(normed_all, tile * d_cols, d_cols, 1)
    weight_in_grad = dot(normed_cols, pre_grad_all, ((0,), (0,))) * grad_scale
    up_cols = lax.dynamic_slice_in_dim(up_all, tile * d_cols, d_cols, 1)
    weight_out_grad = dot(hidden_all, up_cols, ((0,), (0,))) * grad_scale

    def natural(mine, other):
        even = jnp.where(core == 0, mine, other).reshape(tiles, groups // 2, sub, -1)
        odd = jnp.where(core == 0, other, mine).reshape(tiles, groups // 2, sub, -1)
        return jnp.stack([even, odd], axis=2).reshape(tiles, tile_rows, -1)

    out_all = natural(out_mine, out_other)
    offsets_all = natural(packed_mine[..., features:], packed_other[..., features:]).astype(F32)
    rim = jnp.zeros_like(out_all[:1, :HALO])
    before = jnp.concatenate([rim, out_all[:-1, tile_rows - HALO :]], axis=0)
    after = jnp.concatenate([out_all[1:, :HALO], rim], axis=0)
    extended = jnp.concatenate([before, out_all, after], axis=1)
    share = tap_count * features // tiles
    first = (tile * share) // features
    start = tile * share - first * features
    ext_ids = jnp.arange(cells, dtype=F32)[None, None, :]

    def taps_at(k):
        offset = lax.dynamic_slice_in_dim(offsets_all, k, 1, 2)
        target = offset + jnp.arange(tile_rows, dtype=F32)[None, :, None] + HALO
        target = jnp.where(offset == ABSENT, -1.0, target)
        pick = (ext_ids == target).astype(BF)
        picked = lax.dot_general(
            pick, extended, (((2,), (1,)), ((0,), (0,))), preferred_element_type=F32
        )
        return picked.astype(BF).reshape(tiles * tile_rows, features)

    pair = jnp.concatenate([taps_at(first), taps_at(jnp.minimum(first + 1, tap_count - 1))], axis=1)
    own_taps = lax.dynamic_slice_in_dim(pair, start, share, 1)
    grads_all = coarse_grads.reshape(tiles * tile_rows, cols)
    weight_conv_grad = dot(own_taps, grads_all, ((0,), (0,))) * grad_scale
    return (fine_cells, grad_latent, weight_in_grad, weight_out_grad, weight_conv_grad)


def solution(mesh):
    placed = (
        P(("tile", "tp"), None),
        P(None, "tp"),
        P("tp", None),
        P(None, "tp"),
        P("tile", None),
        P(("tile", "tp")),
        P(("tile", "tp"), None),
    )
    return jax.shard_map(
        local,
        mesh=mesh,
        in_specs=placed,
        out_specs=(
            P(("tile", "tp"), None),
            P(("tile", "tp"), None),
            P("tile", "tp"),
            P("tp", "tile"),
            P("tile", "tp"),
        ),
        check_vma=False,
    )
```
